32 devices in a mesh: seq: 8 (over z, x), head: 4 (over y, core).
Axes of the slice: x: 2, y: 2, z: 4, core: 2. Of those that a mesh axis runs over, the one named last changes fastest.
Arguments:
- queries: bfloat16 [4096, 5120], P('seq', 'head'), may hold values from -13 to 13, as said below
- keys: bfloat16 [4096, 1024], P('seq', 'head'), may hold values from -13 to 13, as said below
- values: bfloat16 [4096, 1024], P('seq', 'head'), may hold values from -6 to 6
- out_weight: bfloat16 [5120, 2560], P('head', 'seq'), may hold values from -0.078125 to 0.078125
- d_proj: bfloat16 [4096, 2560], P('seq', 'head'), may hold values from -6 to 6
- block_section: int32 [32], replicated, may hold values from 0 to 3, as said below
- section_parent: int32 [4], replicated, may hold values from -1 to 2, as said below
- xref_owner: int32 [384, 1], P('seq'), may hold values from 0 to 7; in each aligned block of 48 rows (0 to 47, 48 to 95, ...) at most 6 rows name the same one
- xref_block: int32 [32, 12], P('seq'), may hold values from 0 to 3
- xref_valid: int32 [32, 12], P('seq'), may hold values 0 or 1
Outputs:
- projected: bfloat16 [4096, 2560], P('seq', 'head')
- d_queries: bfloat16 [4096, 5120], P('seq', 'head')
- d_keys: bfloat16 [4096, 1024], P('seq', 'head')
- d_values: bfloat16 [4096, 1024], P('seq', 'head')
The draws below stay inside these ranges and needn't reach their ends.
Inputs may be any that keep to these rules, and one draw needn't show every extreme that they name: `queries`: entries of order one; a few rows of larger norm. `keys`: entries of order one; a few rows of larger norm. section_parent[s] is an earlier section for s > 0, and section_parent[0] = -1. `block_section`: sections are runs of consecutive blocks, 2 to 14 blocks each, some section exactly 14; no section begins at a block whose index is a positive multiple of 4. `xref_owner`: among the 48 rows of one device, no owner is named more than 6 times; some owner exactly 6 times.
All inputs are finite; a program needn't handle non-finite values. No bound on the sum of `xref_valid` on one device may be relied on, other than what follows from the above.
Results may differ from the reference program's by a relative error of at most 0.015.
The reference program's roundings to bfloat16 on the way count: a program that leaves them out, or rounds other values in their place, can miss the bound.
Values may be sent and summed in bfloat16 or wider, within the bound.
No kernel may reach another device: no remote copies, remote signals or barrier semaphores. Data moves between devices by JAX's collectives and lax.ppermute only.
A program may use at most 192 MiB of HBM per device.

```python
import math
import jax
import jax.numpy as jnp
import numpy as np
from jax import lax

QUERY_HEAD_COUNT = 40
KEY_VALUE_HEADS = 8
HEAD_DIMENSION = 128
OUTW = 2560
BLK = 128
LOOK = 4
ANC = 2
XREF = 12
BPD = 4
BLOCKS = 32
DOCUMENT_TOKENS = 4096
SECTIONS = 4
CAP = 6
N_SEQ = 8


def draw_queries(key, part):
    dimension_list = (DOCUMENT_TOKENS, QUERY_HEAD_COUNT * HEAD_DIMENSION)
    values_f = jax.random.truncated_normal(jax.random.fold_in(key, 1), -4.5, 4.5, dimension_list, jnp.float32)
    return values_f.astype(jnp.bfloat16)


def draw_keys(key, part):
    dimension_list = (DOCUMENT_TOKENS, KEY_VALUE_HEADS * HEAD_DIMENSION)
    values_f = jax.random.truncated_normal(jax.random.fold_in(key, 2), -4.5, 4.5, dimension_list, jnp.float32)
    return values_f.astype(jnp.bfloat16)


def draw_block_section(key, part):
    offset_table = jnp.array([-3, -2, -1, 1, 2, 3], jnp.int32)
    bound_ids = jnp.arange(SECTIONS - 1, dtype=jnp.int32)
    picked = jax.random.randint(jax.random.fold_in(key, 21), (SECTIONS - 1,), 0, 6, dtype=jnp.int32)
    offsets = jnp.sum(jnp.where(picked[:, None] == jnp.arange(6, dtype=jnp.int32)[None, :], offset_table[None, :], 0), axis=1)
    longest = jax.random.randint(jax.random.fold_in(key, 22), (), 0, SECTIONS - 2, dtype=jnp.int32)
    offsets = jnp.where(bound_ids == longest, -3, jnp.where(bound_ids == longest + 1, 3, offsets))
    starts = 8 * (bound_ids + 1) + offsets
    block_ids = jnp.arange(BLOCKS, dtype=jnp.int32)
    return jnp.sum((block_ids[:, None] >= starts[None, :]).astype(jnp.int32), axis=1).astype(jnp.int32)


def draw_section_parent(key, part):
    section_ids = jnp.arange(SECTIONS, dtype=jnp.int32)
    chosen = jax.random.randint(jax.random.fold_in(key, 5), (SECTIONS,), 0, jnp.maximum(section_ids, 1), dtype=jnp.int32)
    chosen = jnp.where(section_ids == SECTIONS - 1, SECTIONS - 2, chosen)
    return jnp.where(section_ids == 0, -1, chosen).astype(jnp.int32)


def plant(values, key, low, largest):
    longest = values.shape.index(max(values.shape))
    spots = []
    for shift in (0, 1):
        where = [jax.random.randint(jax.random.fold_in(key, axis), (), 0, length) for axis, length in enumerate(values.shape)]
        where[longest] = (where[longest] + shift) % values.shape[longest]
        spots.append(tuple(where))
    return values.at[spots[0]].set(low).at[spots[1]].set(largest)


def levels(stream_key, extent, pieces, smallest, top_value):
    factor_of, own = 1.0, jax.random.fold_in(stream_key, 6)
    for dim, blocks in pieces:
        draws = jnp.exp(jax.random.uniform(jax.random.fold_in(own, dim), (blocks,), jnp.float32, smallest / len(pieces), top_value / len(pieces)))
        factor_of = factor_of * jnp.repeat(draws, extent[dim] // blocks).reshape([-1 if axis == dim else 1 for axis in range(len(extent))])
    return factor_of


def assign_block(key, own, number, rows, count, top, most, lean):
    sequence = jax.random.permutation(key, count)
    heavy_load, ordinary = load_shares(count, rows * top, most, lean, True), load_shares(count, rows * top, most, lean, False)
    places = jnp.arange(count)

    def named(lengths, turn):
        used = int((lengths > 0).sum())
        fixed = max(1, used // 4)
        passed = fixed + (places - fixed + turn * (used - fixed)) % max(1, count - fixed)
        return jnp.zeros((count,), jnp.int32).at[sequence[jnp.where(places < fixed, places, passed)]].set(jnp.asarray(lengths, jnp.int32))

    lengths = jnp.where(number % 4 == 0, named(heavy_load, number // 4), named(ordinary, number - number // 4 - 1))
    mixed = jax.random.permutation(jax.random.fold_in(own, 3), count)
    giver, taker = mixed[0:count // 2 * 2:2], mixed[1:count // 2 * 2:2]
    slack = jnp.minimum(lengths[giver] - 1, most - lengths[taker]) // 2
    slack = jnp.where((giver == sequence[0]) | (taker == sequence[0]) | (lengths[taker] == 0), 0, jnp.maximum(slack, 0))
    passed = jax.random.randint(jax.random.fold_in(own, 4), (count // 2,), 0, 1 << 20) % (slack + 1)
    lengths = lengths.at[giver].add(-passed).at[taker].add(passed)
    items = jnp.searchsorted(jnp.cumsum(lengths), jnp.arange(rows * top), side="right").astype(jnp.int32)
    table = items.reshape(top, rows).T
    table = table[jax.random.permutation(jax.random.fold_in(own, 1), rows)]
    turn = jax.random.randint(jax.random.fold_in(own, 2), (rows, 1), 0, top)
    return jnp.take_along_axis(table, (jnp.arange(top)[None, :] + turn) % top, axis=1)


def load_shares(number_of, total, most, lean, full):
    portions = [(1 << 20) // math.isqrt(rank ** lean) + 1 for rank in range(1, number_of + 1)]
    largest = most if full else min(most, max(-(-total // number_of), total * portions[0] // sum(portions)))
    least = 1 if total - largest >= number_of - 1 else 0
    given, surplus = [largest] + [least] * (number_of - 1), total - largest - least * (number_of - 1)
    while surplus > 0:
        candidates = [i for i in range(1, number_of) if given[i] < largest] or [i for i in range(1, number_of) if given[i] < most]
        whole, remaining = sum([portions[i] for i in candidates]), surplus
        for i in candidates:
            more = min(most - given[i], max(1, remaining * portions[i] // whole), surplus)
            given[i] = given[i] + more
            surplus = surplus - more
    return np.array(given)


def centred(own_key, shape, deviation, reach, shards=(), held_as=jnp.bfloat16):
    drawn = deviation * jax.random.normal(own_key, shape, jnp.float32)
    if shards:
        drawn = drawn * levels(own_key, shape, shards, -0.22, 0.18)
    return jnp.clip(drawn, -reach, reach).astype(held_as)


def setup_inputs(seed: int = 0) -> dict:
    splits = jax.random.split(jax.random.key(seed), 11)
    queries = draw_queries(jax.random.fold_in(splits[10], 71), 0)
    keys = draw_keys(jax.random.fold_in(splits[10], 71), 0)
    values = centred(splits[2], (DOCUMENT_TOKENS, KEY_VALUE_HEADS * HEAD_DIMENSION), 1.0, 6.0, ((0, 8), (1, 4)))
    out_weight = centred(splits[3], (QUERY_HEAD_COUNT * HEAD_DIMENSION, OUTW), (QUERY_HEAD_COUNT * HEAD_DIMENSION) ** -0.5, 0.078125, ((0, 4), (1, 8)))
    d_proj = centred(splits[4], (DOCUMENT_TOKENS, OUTW), 1.0, 6.0, ((0, 8), (1, 4)))
    block_section = draw_block_section(jax.random.fold_in(splits[10], 71), 0)
    section_parent = draw_section_parent(jax.random.fold_in(splits[10], 71), 0)
    xref_owner_keys = jax.random.split(jax.random.fold_in(splits[7], 1), (BLOCKS * XREF) // (BPD * XREF))
    xref_owner_turns = jax.random.permutation(jax.random.fold_in(splits[7], 3), (BLOCKS * XREF) // (BPD * XREF))
    xref_owner = jax.vmap(lambda own, number: assign_block(jax.random.fold_in(splits[7], 2), own, number, BPD * XREF, N_SEQ, 1, CAP, 2))(xref_owner_keys, xref_owner_turns).reshape((BLOCKS * XREF, 1))
    xref_block = plant(jax.random.randint(splits[8], (BLOCKS, XREF), 0, BPD), jax.random.fold_in(splits[8], 1), 0, BPD - 1).astype(jnp.int32)
    xref_valid = plant((jax.random.randint(splits[9], (BLOCKS, XREF), 0, 4) < 3).astype(jnp.int32), jax.random.fold_in(splits[9], 1), 0, 1)
    return {"queries": queries, "keys": keys, "values": values, "out_weight": out_weight, "d_proj": d_proj, "block_section": block_section, "section_parent": section_parent, "xref_owner": xref_owner, "xref_block": xref_block, "xref_valid": xref_valid}


neg_large = -1e+30

def split_queries(block, kv_heads):
    row_count = block.shape[0]
    group_size = block.shape[1] // (HEAD_DIMENSION * kv_heads)
    return block.reshape(row_count, kv_heads, group_size, HEAD_DIMENSION).transpose(1, 2, 0, 3)

def merge_queries(heads):
    kv_heads, group_size, row_count, head_size = heads.shape
    return heads.transpose(2, 0, 1, 3).reshape(row_count, kv_heads * group_size * head_size)

def split_keys(key_set, kv_heads):
    num_blocks, row_count, key_value_width = key_set.shape
    return key_set.reshape(num_blocks * row_count, kv_heads, HEAD_DIMENSION).transpose(1, 0, 2)

def merge_keys(grads, num_blocks):
    kv_heads, flat_len, head_size = grads.shape
    return grads.transpose(1, 0, 2).reshape(num_blocks, flat_len // num_blocks * kv_heads * head_size)

def softmax_weights(scores, allowed):
    masked = jnp.where(allowed, scores, neg_large)
    row_max = lax.optimization_barrier(jnp.max(masked, axis=-1, keepdims=True))
    exponent = jnp.where(allowed, jnp.exp(masked - row_max), 0.0)
    return exponent / lax.optimization_barrier(jnp.sum(exponent, axis=-1, keepdims=True))

def product(form, left, right):
    return jnp.einsum(form, left.astype(jnp.float32), right.astype(jnp.float32), precision=lax.Precision.HIGHEST)

def forward_block(query_block, key_set, value_set, allowed):
    kv_heads = key_set.shape[2] // HEAD_DIMENSION
    scaling = HEAD_DIMENSION ** (-0.5)
    query_heads = split_queries(query_block, kv_heads)
    key_heads = split_keys(key_set, kv_heads)
    value_heads = split_keys(value_set, kv_heads)
    scores = product('cgqd,ckd->cgqk', query_heads, key_heads) * scaling
    weights = softmax_weights(scores, allowed[None, None])
    output = product('cgqk,ckd->cgqd', weights.astype(jnp.bfloat16), value_heads)
    return merge_queries(output).astype(jnp.bfloat16)

def backward_block(query_block, key_set, value_set, allowed, attn, d_attn):
    kv_heads = key_set.shape[2] // HEAD_DIMENSION
    scaling = HEAD_DIMENSION ** (-0.5)
    num_blocks = key_set.shape[0]
    query_heads = split_queries(query_block, kv_heads)
    key_heads = split_keys(key_set, kv_heads)
    value_heads = split_keys(value_set, kv_heads)
    scores = product('cgqd,ckd->cgqk', query_heads, key_heads) * scaling
    weights = softmax_weights(scores, allowed[None, None])
    light = weights.astype(jnp.bfloat16)
    grad_heads = split_queries(d_attn, kv_heads)
    attn_heads = split_queries(attn, kv_heads)
    delta = lax.optimization_barrier(jnp.sum(grad_heads.astype(jnp.float32) * attn_heads.astype(jnp.float32), axis=-1, keepdims=True))
    d_weights = product('cgqd,ckd->cgqk', grad_heads, value_heads)
    d_scores = (weights * (d_weights - delta) * scaling).astype(jnp.bfloat16)
    grad_query = product('cgqk,ckd->cgqd', d_scores, key_heads)
    key_terms = product('cgqk,cgqd->ckd', d_scores, query_heads)
    value_terms = product('cgqk,cgqd->ckd', light, grad_heads)
    return (merge_queries(grad_query).astype(jnp.bfloat16), merge_keys(key_terms, num_blocks), merge_keys(value_terms, num_blocks))

def reference(queries, keys, values, out_weight, d_proj, block_section, section_parent, xref_owner, xref_block, xref_valid):
    key_value_width = KEY_VALUE_HEADS * HEAD_DIMENSION
    blk_width = BLK * key_value_width
    behind = LOOK - 1
    key_count = LOOK + ANC + XREF
    zero = jnp.zeros((), jnp.int32)
    section_ids = jnp.arange(SECTIONS, dtype=jnp.int32)
    member = (section_ids[:, None] == block_section[None, :]).astype(jnp.float32)
    counts = lax.optimization_barrier(jnp.sum(member, axis=1))
    root_counts = jnp.sqrt(counts)

    def summarize(array):
        flat = array.reshape(BLOCKS, blk_width).astype(jnp.float32)
        summed = jnp.dot(member, flat, precision=lax.Precision.HIGHEST) / root_counts[:, None]
        return summed.astype(jnp.bfloat16).reshape(SECTIONS, BLK, key_value_width)
    summary_keys = summarize(keys)
    summary_values = summarize(values)
    chain = [block_section]
    for depth_idx in range(1, ANC):
        prior = chain[-1]
        chain.append(jnp.where(prior >= 0, section_parent[jnp.clip(prior, 0)], -1))
    ancestors = jnp.stack(chain, axis=1)
    targets = xref_owner.reshape(BLOCKS, XREF) * BPD + xref_block
    key_blocks = keys.reshape(BLOCKS, BLK, key_value_width)
    value_blocks = values.reshape(BLOCKS, BLK, key_value_width)
    pad_keys = jnp.concatenate([jnp.zeros((behind, BLK, key_value_width), jnp.bfloat16), key_blocks])
    pad_values = jnp.concatenate([jnp.zeros((behind, BLK, key_value_width), jnp.bfloat16), value_blocks])
    padded_sec = jnp.concatenate([jnp.full((behind,), -1, jnp.int32), block_section])
    positions = jnp.arange(BLK)
    causal = positions[None, :] <= positions[:, None]
    is_last = jnp.arange(LOOK) == LOOK - 1

    def step(carry, block):
        grad_keys, grad_values, up_keys, up_values = carry
        own_keys = lax.dynamic_slice(pad_keys, (block, zero, zero), (LOOK, BLK, key_value_width))
        own_values = lax.dynamic_slice(pad_values, (block, zero, zero), (LOOK, BLK, key_value_width))
        own_sec = lax.dynamic_slice(padded_sec, (block,), (LOOK,))
        chosen_ups = ancestors[block]
        safe_ups = jnp.clip(chosen_ups, 0)
        refs = targets[block]
        key_set = jnp.concatenate([own_keys, summary_keys[safe_ups], key_blocks[refs]], axis=0)
        value_set = jnp.concatenate([own_values, summary_values[safe_ups], value_blocks[refs]], axis=0)
        own_ok = own_sec == block_section[block]
        own_allowed = own_ok[None, :, None] & (jnp.logical_not(is_last)[None, :, None] | causal[:, None, :])
        up_allowed = jnp.broadcast_to((chosen_ups >= 0)[None, :, None], (BLK, ANC, BLK))
        ref_allowed = jnp.broadcast_to((xref_valid[block] > 0)[None, :, None], (BLK, XREF, BLK))
        allowed = jnp.concatenate([own_allowed, up_allowed, ref_allowed], axis=1).reshape(BLK, key_count * BLK)
        query_block = lax.dynamic_slice(queries, (block * BLK, zero), (BLK, QUERY_HEAD_COUNT * HEAD_DIMENSION))
        attn = forward_block(query_block, key_set, value_set, allowed)
        projected = jnp.dot(attn, out_weight, preferred_element_type=jnp.float32).astype(jnp.bfloat16)
        cotangent = lax.dynamic_slice(d_proj, (block * BLK, zero), (BLK, OUTW))
        d_attn = jnp.dot(cotangent, out_weight.T, preferred_element_type=jnp.float32).astype(jnp.bfloat16)
        grad_query, key_terms, value_terms = backward_block(query_block, key_set, value_set, allowed, attn, d_attn)

        def absorb(grads, ups_acc, terms):
            terms = terms.reshape(key_count, BLK, key_value_width)
            window = lax.dynamic_slice(grads, (block, zero, zero), (LOOK, BLK, key_value_width))
            grads = lax.dynamic_update_slice(grads, window + terms[:LOOK], (block, zero, zero))
            ups_acc = ups_acc.at[safe_ups].add(terms[LOOK:LOOK + ANC])
            rounded = lax.optimization_barrier(terms[LOOK + ANC:].astype(jnp.bfloat16)).astype(jnp.float32)
            grads = grads.at[refs + behind].add(rounded)
            return (grads, ups_acc)
        grad_keys, up_keys = absorb(grad_keys, up_keys, key_terms)
        grad_values, up_values = absorb(grad_values, up_values, value_terms)
        return ((grad_keys, grad_values, up_keys, up_values), (projected, grad_query))
    start_grads = jnp.zeros((BLOCKS + behind, BLK, key_value_width), jnp.float32)
    start_ups = jnp.zeros((SECTIONS, BLK, key_value_width), jnp.float32)
    carry, outputs = lax.scan(step, (start_grads, start_grads, start_ups, start_ups), jnp.arange(BLOCKS, dtype=jnp.int32))
    grad_keys, grad_values, up_keys, up_values = carry
    projs, grad_queries = outputs
    spread_down = member.T / root_counts[None, :]

    def finish(grads, ups_acc):
        from_ups = jnp.dot(spread_down, ups_acc.reshape(SECTIONS, blk_width), precision=lax.Precision.HIGHEST)
        return (grads[behind:].reshape(BLOCKS, blk_width) + from_ups).astype(jnp.bfloat16).reshape(DOCUMENT_TOKENS, key_value_width)
    return (projs.reshape(DOCUMENT_TOKENS, OUTW), grad_queries.reshape(DOCUMENT_TOKENS, QUERY_HEAD_COUNT * HEAD_DIMENSION), finish(grad_keys, up_keys), finish(grad_values, up_values))
```

```python
import functools
import math

import jax
import jax.numpy as jnp
from jax import lax
from jax.experimental import pallas as pl
from jax.experimental.pallas import tpu as pltpu
from jax.sharding import PartitionSpec as P

HEAD_DIMENSION = 128
BLK = 128
LOOK = 4
ANC = 2
XREF = 12
SLOTS = LOOK + ANC + XREF
GROUP = 2

neg_large = -1e30
scaling = HEAD_DIMENSION ** (-0.5)
to_base_two = scaling * math.log2(math.e)
vmem_limit = 62 * 1024 * 1024


def rows_of(index):
    return pl.ds(pl.multiple_of(index * BLK, BLK), BLK)


def product(left, right, left_dim, right_dim):
    return lax.dot_general(
        left, right, (((left_dim,), (right_dim,)), ((), ())), preferred_element_type=jnp.float32
    )


def stacked(block_ref, heads):
    return [block_ref[:, g * HEAD_DIMENSION : (g + 1) * HEAD_DIMENSION] for g in range(heads)]


def masked_scores(scores, first_slot, valid_count, heads):
    rows = heads * BLK
    key_minus_query = lax.broadcasted_iota(jnp.int32, (BLK, BLK), 1) - lax.broadcasted_iota(
        jnp.int32, (BLK, BLK), 0
    )
    ahead = jnp.concatenate([key_minus_query] * heads, axis=0)
    pieces = []
    for w in range(GROUP):
        slot = first_slot + w
        reach = jnp.where(slot < valid_count, jnp.where(slot == 0, 0, BLK), -BLK)
        piece = scores[:, w * BLK : (w + 1) * BLK]
        pieces.append(jnp.where(ahead <= reach, piece, neg_large))
    return pieces


def forward_kernel(
    order_ref, count_ref, section_ref, root_ref,
    query_ref, key_ref, value_ref,
    attn_ref, lse_ref, all_keys_ref, all_values_ref,
    stack_ref, score_ref, wide_ref, out_ref, total_ref,
):
    block = pl.program_id(1)
    heads = query_ref.shape[1] // HEAD_DIMENSION
    blocks = key_ref.shape[0] // BLK
    sections = root_ref.shape[0]

    @pl.when(block == 0)
    def _():
        for source, target in ((key_ref, all_keys_ref), (value_ref, all_values_ref)):
            target[0, : blocks * BLK] = source[...]
            total_ref[...] = jnp.zeros_like(total_ref)

            @pl.loop(0, blocks)
            def _(index):
                place = rows_of(section_ref[index])
                total_ref[place] += source[rows_of(index)].astype(jnp.float32)

            @pl.loop(0, sections)
            def _(index):
                target[0, rows_of(blocks + index)] = (
                    total_ref[rows_of(index)] / root_ref[index]
                ).astype(jnp.bfloat16)

    for g, part in enumerate(stacked(query_ref, heads)):
        stack_ref[g * BLK : (g + 1) * BLK] = part
    query = stack_ref[...]
    valid_count = count_ref[block]
    steps = (valid_count + GROUP - 1) // GROUP

    def gathered(source, step):
        return jnp.concatenate(
            [source[0, rows_of(order_ref[block, step * GROUP + w])] for w in range(GROUP)], axis=0
        )

    wide_ref[...] = jnp.full_like(wide_ref, neg_large)

    @pl.loop(0, steps)
    def _(step):
        scores = product(query, gathered(all_keys_ref, step), 1, 1)
        pieces = masked_scores(scores, step * GROUP, valid_count, heads)
        largest = wide_ref[...]
        for w, piece in enumerate(pieces):
            score_ref[step, :, w * BLK : (w + 1) * BLK] = piece
            largest = jnp.maximum(largest, piece)
        wide_ref[...] = largest

    largest = jnp.max(wide_ref[...], axis=1, keepdims=True) * to_base_two
    wide_ref[...] = jnp.zeros_like(wide_ref)

    @pl.loop(0, steps)
    def _(step):
        exponent = jnp.exp2(score_ref[step] * to_base_two - largest)
        score_ref[step] = exponent
        total = wide_ref[...]
        for w in range(GROUP):
            total = total + exponent[:, w * BLK : (w + 1) * BLK]
        wide_ref[...] = total

    total = jnp.sum(wide_ref[...], axis=1, keepdims=True)
    lse_ref[...] = jnp.broadcast_to(largest + jnp.log2(total), lse_ref.shape)
    inverse = 1.0 / total
    out_ref[...] = jnp.zeros_like(out_ref)

    @pl.loop(0, steps)
    def _(step):
        light = (score_ref[step] * inverse).astype(jnp.bfloat16)
        out_ref[...] += product(light, gathered(all_values_ref, step), 1, 0)

    for g in range(heads):
        attn_ref[:, g * HEAD_DIMENSION : (g + 1) * HEAD_DIMENSION] = out_ref[
            g * BLK : (g + 1) * BLK
        ].astype(jnp.bfloat16)


def backward_kernel(
    order_ref, count_ref, section_ref, rounded_ref, root_ref,
    query_ref, grad_ref, attn_ref, lse_ref, all_keys_ref, all_values_ref,
    grad_query_ref, terms_ref,
    query_stack, grad_stack, delta_ref, sum_ref, key_sum_ref, value_sum_ref,
):
    block = pl.program_id(1)
    last = pl.num_programs(1) - 1
    heads = query_ref.shape[1] // HEAD_DIMENSION
    blocks = terms_ref.shape[0] // BLK

    @pl.when(block == 0)
    def _():
        key_sum_ref[...] = jnp.zeros_like(key_sum_ref)
        value_sum_ref[...] = jnp.zeros_like(value_sum_ref)

    for g in range(heads):
        lanes = slice(g * HEAD_DIMENSION, (g + 1) * HEAD_DIMENSION)
        rows = slice(g * BLK, (g + 1) * BLK)
        query_stack[rows] = query_ref[:, lanes]
        grad = grad_ref[:, lanes]
        grad_stack[rows] = grad
        delta = jnp.sum(
            grad.astype(jnp.float32) * attn_ref[:, lanes].astype(jnp.float32), axis=1, keepdims=True
        )
        delta_ref[rows] = jnp.broadcast_to(delta, (BLK, BLK))
    query = query_stack[...]
    grad = grad_stack[...]
    valid_count = count_ref[block]
    steps = (valid_count + GROUP - 1) // GROUP
    sum_ref[...] = jnp.zeros_like(sum_ref)

    @pl.loop(0, steps)
    def _(step):
        places = [order_ref[block, step * GROUP + w] for w in range(GROUP)]
        keys = jnp.concatenate([all_keys_ref[0, rows_of(place)] for place in places], axis=0)
        values = jnp.concatenate([all_values_ref[0, rows_of(place)] for place in places], axis=0)
        scores = product(query, keys, 1, 1)
        d_weights = product(grad, values, 1, 1)
        lse = lse_ref[...]
        delta = delta_ref[...]
        light, d_scores = [], []
        for w, piece in enumerate(masked_scores(scores, step * GROUP, valid_count, heads)):
            weights = jnp.exp2(piece * to_base_two - lse)
            light.append(weights.astype(jnp.bfloat16))
            slope = d_weights[:, w * BLK : (w + 1) * BLK] - delta
            d_scores.append((weights * slope * scaling).astype(jnp.bfloat16))
        light = jnp.concatenate(light, axis=1)
        d_scores = jnp.concatenate(d_scores, axis=1)
        sum_ref[...] += product(d_scores, keys, 1, 0)
        key_terms = product(d_scores, query, 0, 0)
        value_terms = product(light, grad, 0, 0)
        for w, place in enumerate(places):
            rounds = rounded_ref[block, step * GROUP + w] > 0
            for terms, target in ((key_terms, key_sum_ref), (value_terms, value_sum_ref)):
                term = terms[w * BLK : (w + 1) * BLK]
                term = jnp.where(rounds, term.astype(jnp.bfloat16).astype(jnp.float32), term)
                target[rows_of(place)] += term

    for g in range(heads):
        grad_query_ref[:, g * HEAD_DIMENSION : (g + 1) * HEAD_DIMENSION] = sum_ref[
            g * BLK : (g + 1) * BLK
        ].astype(jnp.bfloat16)

    @pl.when(block == last)
    def _():
        @pl.loop(0, blocks)
        def _(index):
            section = section_ref[index]
            root = root_ref[section]
            for half, source in enumerate((key_sum_ref, value_sum_ref)):
                lanes = slice(half * HEAD_DIMENSION, (half + 1) * HEAD_DIMENSION)
                total = source[rows_of(index)] + source[rows_of(blocks + section)] / root
                terms_ref[rows_of(index), lanes] = total.astype(jnp.bfloat16)


def attention_forward(queries, pairs, order, count, block_section, root_counts):
    tokens, width = queries.shape
    kv_heads = pairs.shape[1] // (2 * HEAD_DIMENSION)
    heads = width // (kv_heads * HEAD_DIMENSION)
    blocks, sections = block_section.shape[0], root_counts.shape[0]
    own_blocks = tokens // BLK
    extended = (blocks + sections) * BLK
    rows = heads * BLK
    smem = pl.BlockSpec(memory_space=pltpu.SMEM)
    whole = pl.BlockSpec((1, extended, HEAD_DIMENSION), lambda c, b: (c, 0, 0))
    by_block = pl.BlockSpec((BLK, heads * HEAD_DIMENSION), lambda c, b: (b, c))
    matmul = 2 * tokens * SLOTS * BLK * width
    return pl.pallas_call(
        forward_kernel,
        name="attention_forward",
        grid=(kv_heads, own_blocks),
        in_specs=[
            smem, smem, smem, smem,
            by_block,
            pl.BlockSpec((blocks * BLK, HEAD_DIMENSION), lambda c, b: (0, 2 * c)),
            pl.BlockSpec((blocks * BLK, HEAD_DIMENSION), lambda c, b: (0, 2 * c + 1)),
        ],
        out_specs=[
            by_block,
            pl.BlockSpec((None, None, rows, HEAD_DIMENSION), lambda c, b: (c, b, 0, 0)),
            whole,
            whole,
        ],
        out_shape=[
            jax.ShapeDtypeStruct((tokens, width), jnp.bfloat16),
            jax.ShapeDtypeStruct((kv_heads, own_blocks, rows, HEAD_DIMENSION), jnp.float32),
            jax.ShapeDtypeStruct((kv_heads, extended, HEAD_DIMENSION), jnp.bfloat16),
            jax.ShapeDtypeStruct((kv_heads, extended, HEAD_DIMENSION), jnp.bfloat16),
        ],
        scratch_shapes=[
            pltpu.VMEM((rows, HEAD_DIMENSION), jnp.bfloat16),
            pltpu.VMEM((-(-SLOTS // GROUP), rows, GROUP * BLK), jnp.float32),
            pltpu.VMEM((rows, HEAD_DIMENSION), jnp.float32),
            pltpu.VMEM((rows, HEAD_DIMENSION), jnp.float32),
            pltpu.VMEM((sections * BLK, HEAD_DIMENSION), jnp.float32),
        ],
        compiler_params=pltpu.CompilerParams(vmem_limit_bytes=vmem_limit),
        cost_estimate=pl.CostEstimate(
            flops=2 * matmul, bytes_accessed=8 << 20, transcendentals=matmul // 256
        ),
    )(order, count, block_section, root_counts, queries, pairs, pairs)


def attention_backward(
    queries, d_attn, attn, lse, all_keys, all_values, order, count, rounded, block_section, root_counts
):
    tokens, width = queries.shape
    kv_heads, extended, _ = all_keys.shape
    heads = width // (kv_heads * HEAD_DIMENSION)
    blocks = block_section.shape[0]
    own_blocks = tokens // BLK
    rows = heads * BLK
    smem = pl.BlockSpec(memory_space=pltpu.SMEM)
    whole = pl.BlockSpec((1, extended, HEAD_DIMENSION), lambda c, b: (c, 0, 0))
    by_block = pl.BlockSpec((BLK, heads * HEAD_DIMENSION), lambda c, b: (b, c))
    matmul = 2 * tokens * SLOTS * BLK * width
    return pl.pallas_call(
        backward_kernel,
        name="attention_backward",
        grid=(kv_heads, own_blocks),
        in_specs=[
            smem, smem, smem, smem, smem,
            by_block, by_block, by_block,
            pl.BlockSpec((None, None, rows, HEAD_DIMENSION), lambda c, b: (c, b, 0, 0)),
            whole, whole,
        ],
        out_specs=[
            by_block,
            pl.BlockSpec((blocks * BLK, 2 * HEAD_DIMENSION), lambda c, b: (0, c)),
        ],
        out_shape=[
            jax.ShapeDtypeStruct((tokens, width), jnp.bfloat16),
            jax.ShapeDtypeStruct((blocks * BLK, kv_heads * 2 * HEAD_DIMENSION), jnp.bfloat16),
        ],
        scratch_shapes=[
            pltpu.VMEM((rows, HEAD_DIMENSION), jnp.bfloat16),
            pltpu.VMEM((rows, HEAD_DIMENSION), jnp.bfloat16),
            pltpu.VMEM((rows, HEAD_DIMENSION), jnp.float32),
            pltpu.VMEM((rows, HEAD_DIMENSION), jnp.float32),
            pltpu.VMEM((extended, HEAD_DIMENSION), jnp.float32),
            pltpu.VMEM((extended, HEAD_DIMENSION), jnp.float32),
        ],
        compiler_params=pltpu.CompilerParams(vmem_limit_bytes=vmem_limit),
        cost_estimate=pl.CostEstimate(
            flops=5 * matmul, bytes_accessed=16 << 20, transcendentals=matmul // 256
        ),
    )(
        order, count, block_section, rounded, root_counts,
        queries, d_attn, attn, lse, all_keys, all_values,
    )


def key_slots(block_section, section_parent, xref_owner, xref_block, xref_valid, first_blk):
    blocks = block_section.shape[0]
    blk_count = xref_block.shape[0]
    own = first_blk + jnp.arange(blk_count, dtype=jnp.int32)
    offsets = jnp.concatenate([jnp.array([0], jnp.int32), jnp.arange(1 - LOOK, 0, dtype=jnp.int32)])
    window = own[:, None] + offsets[None, :]
    is_block = jnp.arange(blocks, dtype=jnp.int32)

    def section_of(index):
        return jnp.sum(
            jnp.where(index[..., None] == is_block, block_section + 1, 0), axis=-1
        ) - 1

    my_sec = section_of(own)
    window_ok = section_of(window) == my_sec[:, None]
    chain = [my_sec]
    is_section = jnp.arange(section_parent.shape[0], dtype=jnp.int32)
    for _ in range(ANC - 1):
        prior = chain[-1]
        chain.append(
            jnp.sum(jnp.where(prior[:, None] == is_section, section_parent + 1, 0), axis=1) - 1
        )
    ancestors = jnp.stack(chain, axis=1)
    targets = xref_owner.reshape(blk_count, XREF) * blk_count + xref_block
    place = jnp.concatenate(
        [jnp.maximum(window, 0), blocks + jnp.maximum(ancestors, 0), targets], axis=1
    )
    valid = jnp.concatenate([window_ok, ancestors >= 0, xref_valid > 0], axis=1)
    slot = jnp.arange(SLOTS, dtype=jnp.int32)
    earlier = slot[:, None] < slot[None, :]
    before = jnp.sum(jnp.where(earlier[None], valid[:, :, None].astype(jnp.int32), 0), axis=1)
    count = jnp.sum(valid.astype(jnp.int32), axis=1)
    rank = jnp.where(valid, before, count[:, None] + slot - before)
    sorted_from = rank[:, :, None] == slot
    padded = -(-SLOTS // GROUP) * GROUP - SLOTS
    order = jnp.sum(jnp.where(sorted_from, place[:, :, None], 0), axis=1)
    is_ref = (slot >= LOOK + ANC).astype(jnp.int32)
    rounded = jnp.sum(jnp.where(sorted_from, is_ref[None, :, None], 0), axis=1)
    order, rounded = (jnp.pad(table, ((0, 0), (0, padded))) for table in (order, rounded))
    return order, rounded, count


def exchanged(block, axis, bit):
    size = lax.axis_size(axis)
    return lax.ppermute(block, axis, [(i, i ^ bit) for i in range(size)])


def gathered_by_exchange(block, axis):
    parts = block[None]
    bit = 1
    while bit < lax.axis_size(axis):
        parts = jnp.concatenate([parts, exchanged(parts, axis, bit)], axis=0)
        bit *= 2
    return parts


def cotangent_kernel(me_ref, left_ref, right_ref, out_ref, sum_ref):
    step = pl.program_id(0)

    @pl.when(step == 0)
    def _():
        sum_ref[...] = jnp.zeros_like(sum_ref)

    sum_ref[...] += product(left_ref[...], right_ref[...], 1, 0)

    @pl.when(step == pl.num_programs(0) - 1)
    def _():
        out_ref[...] = sum_ref[...].astype(jnp.bfloat16)


def cotangent_of_attn(parts, weight, me):
    count, tokens, part_width = parts.shape
    width = weight.shape[1]
    return pl.pallas_call(
        cotangent_kernel,
        name="cotangent_of_attn",
        grid_spec=pltpu.PrefetchScalarGridSpec(
            num_scalar_prefetch=1,
            grid=(count,),
            in_specs=[
                pl.BlockSpec((None, tokens, part_width), lambda j, me: (j, 0, 0)),
                pl.BlockSpec((part_width, width), lambda j, me: (me[0] ^ j, 0)),
            ],
            out_specs=pl.BlockSpec((tokens, width), lambda j, me: (0, 0)),
            scratch_shapes=[pltpu.VMEM((tokens, width), jnp.float32)],
        ),
        out_shape=jax.ShapeDtypeStruct((tokens, width), jnp.bfloat16),
        compiler_params=pltpu.CompilerParams(vmem_limit_bytes=vmem_limit),
        cost_estimate=pl.CostEstimate(
            flops=2 * count * tokens * part_width * width,
            bytes_accessed=2 * (parts.size + weight.size + tokens * width),
            transcendentals=0,
        ),
    )(me.reshape(1), parts, weight)


def projection_kernel(attn_ref, weight_ref, out_ref):
    out_ref[...] = product(attn_ref[...], weight_ref[...], 1, 1).astype(jnp.bfloat16)


def projection_parts(attn, weight, count):
    tokens, width = attn.shape
    part_width = weight.shape[0] // count
    return pl.pallas_call(
        projection_kernel,
        name="projection_parts",
        grid=(count,),
        in_specs=[
            pl.BlockSpec((tokens, width), lambda j: (0, 0)),
            pl.BlockSpec((part_width, width), lambda j: (j, 0)),
        ],
        out_specs=pl.BlockSpec((None, tokens, part_width), lambda j: (j, 0, 0)),
        out_shape=jax.ShapeDtypeStruct((count, tokens, part_width), jnp.bfloat16),
        compiler_params=pltpu.CompilerParams(vmem_limit_bytes=vmem_limit),
        cost_estimate=pl.CostEstimate(
            flops=2 * count * tokens * part_width * width,
            bytes_accessed=2 * (attn.size + weight.size + tokens * weight.shape[0]),
            transcendentals=0,
        ),
    )(attn, weight)


def on_device(
    queries,
    keys,
    values,
    out_weight,
    d_proj,
    block_section,
    section_parent,
    xref_owner,
    xref_block,
    xref_valid,
):
    tok_local = queries.shape[0]
    blk_count = tok_local // BLK
    kv_heads = keys.shape[1] // HEAD_DIMENSION
    head_count = lax.axis_size("head")
    first_blk = lax.axis_index("seq") * blk_count

    def columns(array, index):
        return array[:, index * HEAD_DIMENSION : (index + 1) * HEAD_DIMENSION]

    own_pairs = jnp.concatenate(
        [columns(array, c) for c in range(kv_heads) for array in (keys, values)], axis=1
    )
    pairs = lax.all_gather(own_pairs, "seq", axis=0, tiled=True)
    weight = lax.all_gather(out_weight.T, "seq", axis=0, tiled=True)
    d_parts = gathered_by_exchange(d_proj, "head")

    section_ids = jnp.arange(section_parent.shape[0], dtype=jnp.int32)
    root_counts = jnp.sqrt(
        jnp.sum((block_section[:, None] == section_ids[None, :]).astype(jnp.float32), axis=0)
    )
    order, rounded, count = key_slots(
        block_section, section_parent, xref_owner, xref_block, xref_valid, first_blk
    )
    attn, lse, all_keys, all_values = attention_forward(
        queries, pairs, order, count, block_section, root_counts
    )
    d_attn = cotangent_of_attn(d_parts, weight, lax.axis_index("head"))
    parts = projection_parts(attn, weight, head_count)
    projected = lax.psum_scatter(parts, "head", scatter_dimension=0, tiled=False)
    grad_queries, terms = attention_backward(
        queries, d_attn, attn, lse, all_keys, all_values,
        order, count, rounded, block_section, root_counts,
    )
    own_terms = lax.psum_scatter(terms, "seq", scatter_dimension=0, tiled=True)
    d_keys = jnp.concatenate([columns(own_terms, 2 * c) for c in range(kv_heads)], axis=1)
    d_values = jnp.concatenate([columns(own_terms, 2 * c + 1) for c in range(kv_heads)], axis=1)
    return (projected, grad_queries, d_keys, d_values)


def solution(mesh):
    placed = (
        P("seq", "head"),
        P("seq", "head"),
        P("seq", "head"),
        P("head", "seq"),
        P("seq", "head"),
        P(),
        P(),
        P("seq", None),
        P("seq", None),
        P("seq", None),
    )
    return jax.shard_map(
        on_device,
        mesh=mesh,
        in_specs=placed,
        out_specs=(P("seq", "head"), P("seq", "head"), P("seq", "head"), P("seq", "head")),
        check_vma=False,
    )
```

```python
import functools
import math

import jax
import jax.numpy as jnp
from jax import lax
from jax.experimental import pallas as pl
from jax.experimental.pallas import tpu as pltpu
from jax.sharding import PartitionSpec as P

HEAD_DIMENSION = 128
BLK = 128
LOOK = 4
ANC = 2
XREF = 12
SLOTS = LOOK + ANC + XREF
GROUP = 2

neg_large = -1e30
scaling = HEAD_DIMENSION ** (-0.5)
to_base_two = scaling * math.log2(math.e)
vmem_limit = 62 * 1024 * 1024


def rows_of(index):
    return pl.ds(pl.multiple_of(index * BLK, BLK), BLK)


def product(left, right, left_dim, right_dim):
    return lax.dot_general(
        left, right, (((left_dim,), (right_dim,)), ((), ())), preferred_element_type=jnp.float32
    )


def stacked(block_ref, heads):
    return [block_ref[:, g * HEAD_DIMENSION : (g + 1) * HEAD_DIMENSION] for g in range(heads)]


def masked_scores(scores, first_slot, valid_count, heads):
    rows = heads * BLK
    key_minus_query = lax.broadcasted_iota(jnp.int32, (BLK, BLK), 1) - lax.broadcasted_iota(
        jnp.int32, (BLK, BLK), 0
    )
    ahead = jnp.concatenate([key_minus_query] * heads, axis=0)
    pieces = []
    for w in range(GROUP):
        slot = first_slot + w
        reach = jnp.where(slot < valid_count, jnp.where(slot == 0, 0, BLK), -BLK)
        piece = scores[:, w * BLK : (w + 1) * BLK]
        pieces.append(jnp.where(ahead <= reach, piece, neg_large))
    return pieces


def forward_kernel(shard_rows, *refs):
    order_ref, count_ref, section_ref, root_ref, place_ref, query_ref = refs[:6]
    shard_refs = refs[6 : 6 + len(shard_rows)]
    (attn_ref, lse_ref, all_keys_ref, all_values_ref,
     stack_ref, score_ref, wide_ref, out_ref, total_ref) = refs[6 + len(shard_rows) :]
    block = pl.program_id(0)
    heads = query_ref.shape[1] // HEAD_DIMENSION
    blocks = section_ref.shape[0]
    sections = root_ref.shape[0]

    @pl.when(block == 0)
    def _():
        for half, target in enumerate((all_keys_ref, all_values_ref)):
            lanes = slice(half * HEAD_DIMENSION, (half + 1) * HEAD_DIMENSION)
            for number, (shard_ref, rows) in enumerate(zip(shard_refs, shard_rows)):
                first = pl.multiple_of(place_ref[number], BLK)
                target[pl.ds(first, rows)] = shard_ref[:, lanes]
            total_ref[...] = jnp.zeros_like(total_ref)

            @pl.loop(0, blocks)
            def _(index):
                place = rows_of(section_ref[index])
                total_ref[place] += target[rows_of(index)].astype(jnp.float32)

            @pl.loop(0, sections)
            def _(index):
                target[rows_of(blocks + index)] = (
                    total_ref[rows_of(index)] / root_ref[index]
                ).astype(jnp.bfloat16)

    for g, part in enumerate(stacked(query_ref, heads)):
        stack_ref[g * BLK : (g + 1) * BLK] = part
    query = stack_ref[...]
    valid_count = count_ref[block]
    steps = (valid_count + GROUP - 1) // GROUP

    def gathered(source, step):
        return jnp.concatenate(
            [source[rows_of(order_ref[block, step * GROUP + w])] for w in range(GROUP)], axis=0
        )

    wide_ref[...] = jnp.full_like(wide_ref, neg_large)

    @pl.loop(0, steps)
    def _(step):
        scores = product(query, gathered(all_keys_ref, step), 1, 1)
        pieces = masked_scores(scores, step * GROUP, valid_count, heads)
        largest = wide_ref[...]
        for w, piece in enumerate(pieces):
            score_ref[step, :, w * BLK : (w + 1) * BLK] = piece
            largest = jnp.maximum(largest, piece)
        wide_ref[...] = largest

    largest = jnp.max(wide_ref[...], axis=1, keepdims=True) * to_base_two
    wide_ref[...] = jnp.zeros_like(wide_ref)

    @pl.loop(0, steps)
    def _(step):
        exponent = jnp.exp2(score_ref[step] * to_base_two - largest)
        score_ref[step] = exponent
        total = wide_ref[...]
        for w in range(GROUP):
            total = total + exponent[:, w * BLK : (w + 1) * BLK]
        wide_ref[...] = total

    total = jnp.sum(wide_ref[...], axis=1, keepdims=True)
    lse_ref[...] = jnp.broadcast_to(largest + jnp.log2(total), lse_ref.shape)
    inverse = 1.0 / total
    out_ref[...] = jnp.zeros_like(out_ref)

    @pl.loop(0, steps)
    def _(step):
        light = (score_ref[step] * inverse).astype(jnp.bfloat16)
        out_ref[...] += product(light, gathered(all_values_ref, step), 1, 0)

    for g in range(heads):
        attn_ref[:, g * HEAD_DIMENSION : (g + 1) * HEAD_DIMENSION] = out_ref[
            g * BLK : (g + 1) * BLK
        ].astype(jnp.bfloat16)


def backward_kernel(
    order_ref, count_ref, section_ref, rounded_ref, root_ref,
    query_ref, grad_ref, attn_ref, lse_ref, all_keys_ref, all_values_ref,
    grad_query_ref, terms_ref,
    query_stack, grad_stack, delta_ref, sum_ref, key_sum_ref, value_sum_ref,
):
    block = pl.program_id(0)
    last = pl.num_programs(0) - 1
    heads = query_ref.shape[1] // HEAD_DIMENSION
    blocks = terms_ref.shape[0] // BLK

    @pl.when(block == 0)
    def _():
        key_sum_ref[...] = jnp.zeros_like(key_sum_ref)
        value_sum_ref[...] = jnp.zeros_like(value_sum_ref)

    for g in range(heads):
        lanes = slice(g * HEAD_DIMENSION, (g + 1) * HEAD_DIMENSION)
        rows = slice(g * BLK, (g + 1) * BLK)
        query_stack[rows] = query_ref[:, lanes]
        grad = grad_ref[:, lanes]
        grad_stack[rows] = grad
        delta = jnp.sum(
            grad.astype(jnp.float32) * attn_ref[:, lanes].astype(jnp.float32), axis=1, keepdims=True
        )
        delta_ref[rows] = jnp.broadcast_to(delta, (BLK, BLK))
    query = query_stack[...]
    grad = grad_stack[...]
    valid_count = count_ref[block]
    steps = (valid_count + GROUP - 1) // GROUP
    sum_ref[...] = jnp.zeros_like(sum_ref)

    @pl.loop(0, steps)
    def _(step):
        places = [order_ref[block, step * GROUP + w] for w in range(GROUP)]
        keys = jnp.concatenate([all_keys_ref[rows_of(place)] for place in places], axis=0)
        values = jnp.concatenate([all_values_ref[rows_of(place)] for place in places], axis=0)
        scores = product(query, keys, 1, 1)
        d_weights = product(grad, values, 1, 1)
        lse = lse_ref[...]
        delta = delta_ref[...]
        light, d_scores = [], []
        for w, piece in enumerate(masked_scores(scores, step * GROUP, valid_count, heads)):
            weights = jnp.exp2(piece * to_base_two - lse)
            light.append(weights.astype(jnp.bfloat16))
            slope = d_weights[:, w * BLK : (w + 1) * BLK] - delta
            d_scores.append((weights * slope * scaling).astype(jnp.bfloat16))
        light = jnp.concatenate(light, axis=1)
        d_scores = jnp.concatenate(d_scores, axis=1)
        sum_ref[...] += product(d_scores, keys, 1, 0)
        key_terms = product(d_scores, query, 0, 0)
        value_terms = product(light, grad, 0, 0)
        for w, place in enumerate(places):
            rounds = rounded_ref[block, step * GROUP + w] > 0
            for terms, target in ((key_terms, key_sum_ref), (value_terms, value_sum_ref)):
                term = terms[w * BLK : (w + 1) * BLK]
                term = jnp.where(rounds, term.astype(jnp.bfloat16).astype(jnp.float32), term)
                target[rows_of(place)] += term

    for g in range(heads):
        grad_query_ref[:, g * HEAD_DIMENSION : (g + 1) * HEAD_DIMENSION] = sum_ref[
            g * BLK : (g + 1) * BLK
        ].astype(jnp.bfloat16)

    @pl.when(block == last)
    def _():
        @pl.loop(0, blocks)
        def _(index):
            section = section_ref[index]
            root = root_ref[section]
            for half, source in enumerate((key_sum_ref, value_sum_ref)):
                lanes = slice(half * HEAD_DIMENSION, (half + 1) * HEAD_DIMENSION)
                total = source[rows_of(index)] + source[rows_of(blocks + section)] / root
                terms_ref[rows_of(index), lanes] = total.astype(jnp.bfloat16)


def attention_forward(queries, head, kv_heads, shards, places, order, count, block_section, root_counts):
    tokens = queries.shape[0]
    width = queries.shape[1] // kv_heads
    blocks, sections = block_section.shape[0], root_counts.shape[0]
    own_blocks = tokens // BLK
    extended = (blocks + sections) * BLK
    rows = width // HEAD_DIMENSION * BLK
    smem = pl.BlockSpec(memory_space=pltpu.SMEM)
    whole = pl.BlockSpec((extended, HEAD_DIMENSION), lambda b: (0, 0))
    matmul = 2 * tokens * SLOTS * BLK * width
    return pl.pallas_call(
        functools.partial(forward_kernel, [shard.shape[0] for shard in shards]),
        name="attention_forward",
        grid=(own_blocks,),
        in_specs=[
            smem, smem, smem, smem, smem,
            pl.BlockSpec((BLK, width), lambda b: (b, head)),
            *[pl.BlockSpec(shard.shape, lambda b: (0, 0)) for shard in shards],
        ],
        out_specs=[
            pl.BlockSpec((BLK, width), lambda b: (b, 0)),
            pl.BlockSpec((None, rows, HEAD_DIMENSION), lambda b: (b, 0, 0)),
            whole,
            whole,
        ],
        out_shape=[
            jax.ShapeDtypeStruct((tokens, width), jnp.bfloat16),
            jax.ShapeDtypeStruct((own_blocks, rows, HEAD_DIMENSION), jnp.float32),
            jax.ShapeDtypeStruct((extended, HEAD_DIMENSION), jnp.bfloat16),
            jax.ShapeDtypeStruct((extended, HEAD_DIMENSION), jnp.bfloat16),
        ],
        scratch_shapes=[
            pltpu.VMEM((rows, HEAD_DIMENSION), jnp.bfloat16),
            pltpu.VMEM((-(-SLOTS // GROUP), rows, GROUP * BLK), jnp.float32),
            pltpu.VMEM((rows, HEAD_DIMENSION), jnp.float32),
            pltpu.VMEM((rows, HEAD_DIMENSION), jnp.float32),
            pltpu.VMEM((sections * BLK, HEAD_DIMENSION), jnp.float32),
        ],
        compiler_params=pltpu.CompilerParams(vmem_limit_bytes=vmem_limit),
        cost_estimate=pl.CostEstimate(
            flops=2 * matmul, bytes_accessed=8 << 20, transcendentals=matmul // 256
        ),
    )(order, count, block_section, root_counts, places, queries, *shards)


def attention_backward(
    queries, head, d_attn, attn, lse, all_keys, all_values, order, count, rounded, block_section, root_counts
):
    tokens, width = attn.shape
    extended, _ = all_keys.shape
    blocks = block_section.shape[0]
    own_blocks = tokens // BLK
    rows = width // HEAD_DIMENSION * BLK
    smem = pl.BlockSpec(memory_space=pltpu.SMEM)
    whole = pl.BlockSpec((extended, HEAD_DIMENSION), lambda b: (0, 0))
    by_block = pl.BlockSpec((BLK, width), lambda b: (b, 0))
    matmul = 2 * tokens * SLOTS * BLK * width
    return pl.pallas_call(
        backward_kernel,
        name="attention_backward",
        grid=(own_blocks,),
        in_specs=[
            smem, smem, smem, smem, smem,
            pl.BlockSpec((BLK, width), lambda b: (b, head)),
            pl.BlockSpec((BLK, width), lambda b: (b, head)),
            by_block,
            pl.BlockSpec((None, rows, HEAD_DIMENSION), lambda b: (b, 0, 0)),
            whole, whole,
        ],
        out_specs=[
            by_block,
            pl.BlockSpec((blocks * BLK, 2 * HEAD_DIMENSION), lambda b: (0, 0)),
        ],
        out_shape=[
            jax.ShapeDtypeStruct((tokens, width), jnp.bfloat16),
            jax.ShapeDtypeStruct((blocks * BLK, 2 * HEAD_DIMENSION), jnp.bfloat16),
        ],
        scratch_shapes=[
            pltpu.VMEM((rows, HEAD_DIMENSION), jnp.bfloat16),
            pltpu.VMEM((rows, HEAD_DIMENSION), jnp.bfloat16),
            pltpu.VMEM((rows, HEAD_DIMENSION), jnp.float32),
            pltpu.VMEM((rows, HEAD_DIMENSION), jnp.float32),
            pltpu.VMEM((extended, HEAD_DIMENSION), jnp.float32),
            pltpu.VMEM((extended, HEAD_DIMENSION), jnp.float32),
        ],
        compiler_params=pltpu.CompilerParams(vmem_limit_bytes=vmem_limit),
        cost_estimate=pl.CostEstimate(
            flops=5 * matmul, bytes_accessed=16 << 20, transcendentals=matmul // 256
        ),
    )(
        order, count, block_section, rounded, root_counts,
        queries, d_attn, attn, lse, all_keys, all_values,
    )


class Ring:
    def __init__(self, axis):
        self.axis = axis
        self.size = size = lax.axis_size(axis)
        self.cycle = [*range(0, size, 2), *reversed(range(1, size, 2))]
        at = [self.cycle.index(i) for i in range(size)]
        self.position = jnp.array(at, jnp.int32)[lax.axis_index(axis)]
        self.table = jnp.array(self.cycle, jnp.int32)

    def index_at(self, distance):
        return self.table[(self.position + distance) % self.size]

    def sent(self, block, direction):
        cycle, size = self.cycle, self.size
        route = [(cycle[k], cycle[(k + direction) % size]) for k in range(size)]
        return lax.ppermute(block, self.axis, route)

    def gathered(self, block):
        rows, half = block.shape[0], block.shape[0] // 2
        pieces, firsts = [block], [self.index_at(0) * rows]
        ahead, back = block, block
        for step in range(1, self.size // 2):
            ahead, back = self.sent(ahead, 1), self.sent(back, -1)
            pieces += [ahead, back]
            firsts += [self.index_at(-step) * rows, self.index_at(step) * rows]
        far = self.index_at(self.size // 2) * rows
        pieces += [self.sent(ahead[:half], 1), self.sent(back[half:], -1)]
        firsts += [far, far + half]
        return pieces, jnp.stack(firsts)

    def reduced(self, terms):
        rows = terms.shape[0] // self.size
        half = rows // 2

        def chunk(distance):
            return lax.dynamic_slice_in_dim(terms, self.index_at(distance) * rows, rows)

        def added(*arrays):
            return sum(array.astype(jnp.float32) for array in arrays).astype(jnp.bfloat16)

        far = chunk(self.size // 2)
        ahead, back = self.sent(far[:half], 1), self.sent(far[half:], -1)
        for step in range(self.size // 2 - 1, 0, -1):
            up, down = chunk(step), chunk(-step)
            if step == self.size // 2 - 1:
                ahead = jnp.concatenate([added(up[:half], ahead), up[half:]])
                back = jnp.concatenate([down[:half], added(down[half:], back)])
            else:
                ahead, back = added(up, ahead), added(down, back)
            ahead, back = self.sent(ahead, 1), self.sent(back, -1)
        return added(chunk(0), ahead, back)


def key_slots(block_section, section_parent, xref_owner, xref_block, xref_valid, first_blk):
    blocks = block_section.shape[0]
    blk_count = xref_block.shape[0]
    own = first_blk + jnp.arange(blk_count, dtype=jnp.int32)
    offsets = jnp.concatenate([jnp.array([0], jnp.int32), jnp.arange(1 - LOOK, 0, dtype=jnp.int32)])
    window = own[:, None] + offsets[None, :]
    is_block = jnp.arange(blocks, dtype=jnp.int32)

    def section_of(index):
        return jnp.sum(
            jnp.where(index[..., None] == is_block, block_section + 1, 0), axis=-1
        ) - 1

    my_sec = section_of(own)
    window_ok = section_of(window) == my_sec[:, None]
    chain = [my_sec]
    is_section = jnp.arange(section_parent.shape[0], dtype=jnp.int32)
    for _ in range(ANC - 1):
        prior = chain[-1]
        chain.append(
            jnp.sum(jnp.where(prior[:, None] == is_section, section_parent + 1, 0), axis=1) - 1
        )
    ancestors = jnp.stack(chain, axis=1)
    targets = xref_owner.reshape(blk_count, XREF) * blk_count + xref_block
    place = jnp.concatenate(
        [jnp.maximum(window, 0), blocks + jnp.maximum(ancestors, 0), targets], axis=1
    )
    valid = jnp.concatenate([window_ok, ancestors >= 0, xref_valid > 0], axis=1)
    slot = jnp.arange(SLOTS, dtype=jnp.int32)
    earlier = slot[:, None] < slot[None, :]
    before = jnp.sum(jnp.where(earlier[None], valid[:, :, None].astype(jnp.int32), 0), axis=1)
    count = jnp.sum(valid.astype(jnp.int32), axis=1)
    rank = jnp.where(valid, before, count[:, None] + slot - before)
    sorted_from = rank[:, :, None] == slot
    padded = -(-SLOTS // GROUP) * GROUP - SLOTS
    order = jnp.sum(jnp.where(sorted_from, place[:, :, None], 0), axis=1)
    is_ref = (slot >= LOOK + ANC).astype(jnp.int32)
    rounded = jnp.sum(jnp.where(sorted_from, is_ref[None, :, None], 0), axis=1)
    order, rounded = (jnp.pad(table, ((0, 0), (0, padded))) for table in (order, rounded))
    return order, rounded, count


def exchanged(block, axis, bit):
    size = lax.axis_size(axis)
    return lax.ppermute(block, axis, [(i, i ^ bit) for i in range(size)])


def gathered_by_exchange(block, axis):
    parts = block[None]
    bit = 1
    while bit < lax.axis_size(axis):
        parts = jnp.concatenate([parts, exchanged(parts, axis, bit)], axis=0)
        bit *= 2
    return parts


def reduced_by_exchange(parts, axis):
    bit = lax.axis_size(axis) // 2
    while bit:
        kept, given = parts[:bit], exchanged(parts[bit:], axis, bit)
        parts = (kept.astype(jnp.float32) + given.astype(jnp.float32)).astype(jnp.bfloat16)
        bit //= 2
    return parts[0]


def cotangent_kernel(me_ref, left_ref, right_ref, out_ref, sum_ref):
    step = pl.program_id(0)

    @pl.when(step == 0)
    def _():
        sum_ref[...] = jnp.zeros_like(sum_ref)

    sum_ref[...] += product(left_ref[...], right_ref[...], 1, 0)

    @pl.when(step == pl.num_programs(0) - 1)
    def _():
        out_ref[...] = sum_ref[...].astype(jnp.bfloat16)


def cotangent_of_attn(parts, weight, me):
    count, tokens, part_width = parts.shape
    width = weight.shape[1]
    return pl.pallas_call(
        cotangent_kernel,
        name="cotangent_of_attn",
        grid_spec=pltpu.PrefetchScalarGridSpec(
            num_scalar_prefetch=1,
            grid=(count,),
            in_specs=[
                pl.BlockSpec((None, tokens, part_width), lambda j, me: (j, 0, 0)),
                pl.BlockSpec((part_width, width), lambda j, me: (me[0] ^ j, 0)),
            ],
            out_specs=pl.BlockSpec((tokens, width), lambda j, me: (0, 0)),
            scratch_shapes=[pltpu.VMEM((tokens, width), jnp.float32)],
        ),
        out_shape=jax.ShapeDtypeStruct((tokens, width), jnp.bfloat16),
        compiler_params=pltpu.CompilerParams(vmem_limit_bytes=vmem_limit),
        cost_estimate=pl.CostEstimate(
            flops=2 * count * tokens * part_width * width,
            bytes_accessed=2 * (parts.size + weight.size + tokens * width),
            transcendentals=0,
        ),
    )(me.reshape(1), parts, weight)


def projection_kernel(me_ref, attn_ref, weight_ref, out_ref):
    out_ref[...] = product(attn_ref[...], weight_ref[...], 1, 1).astype(jnp.bfloat16)


def projection_parts(attn, weight, count, me):
    tokens, width = attn.shape
    part_width = weight.shape[0] // count
    return pl.pallas_call(
        projection_kernel,
        name="projection_parts",
        grid_spec=pltpu.PrefetchScalarGridSpec(
            num_scalar_prefetch=1,
            grid=(count,),
            in_specs=[
                pl.BlockSpec((tokens, width), lambda j, me: (0, 0)),
                pl.BlockSpec((part_width, width), lambda j, me: (me[0] ^ j, 0)),
            ],
            out_specs=pl.BlockSpec((None, tokens, part_width), lambda j, me: (j, 0, 0)),
        ),
        out_shape=jax.ShapeDtypeStruct((count, tokens, part_width), jnp.bfloat16),
        compiler_params=pltpu.CompilerParams(vmem_limit_bytes=vmem_limit),
        cost_estimate=pl.CostEstimate(
            flops=2 * count * tokens * part_width * width,
            bytes_accessed=2 * (attn.size + weight.size + tokens * weight.shape[0]),
            transcendentals=0,
        ),
    )(me.reshape(1), attn, weight)


def on_device(
    queries,
    keys,
    values,
    out_weight,
    d_proj,
    block_section,
    section_parent,
    xref_owner,
    xref_block,
    xref_valid,
):
    tok_local = queries.shape[0]
    blk_count = tok_local // BLK
    kv_heads = keys.shape[1] // HEAD_DIMENSION
    head_count = lax.axis_size("head")
    first_blk = lax.axis_index("seq") * blk_count

    def columns(array, index):
        return array[:, index * HEAD_DIMENSION : (index + 1) * HEAD_DIMENSION]

    ring = Ring("seq")
    gathers = [
        ring.gathered(jnp.concatenate([columns(keys, c), columns(values, c)], axis=1))
        for c in range(kv_heads)
    ]
    weight = lax.all_gather(out_weight.T, "seq", axis=0, tiled=True)
    d_parts = gathered_by_exchange(d_proj, "head")

    section_ids = jnp.arange(section_parent.shape[0], dtype=jnp.int32)
    root_counts = jnp.sqrt(
        jnp.sum((block_section[:, None] == section_ids[None, :]).astype(jnp.float32), axis=0)
    )
    order, rounded, count = key_slots(
        block_section, section_parent, xref_owner, xref_block, xref_valid, first_blk
    )
    tables = (block_section, root_counts)
    forward = [
        attention_forward(queries, c, kv_heads, *gathers[c], order, count, *tables)
        for c in range(kv_heads)
    ]
    d_attn = cotangent_of_attn(d_parts, weight, lax.axis_index("head"))
    attn = jnp.concatenate([forward[c][0] for c in range(kv_heads)], axis=1)
    parts = projection_parts(attn, weight, head_count, lax.axis_index("head"))
    projected = reduced_by_exchange(parts, "head")
    grad_queries, grad_keys, grad_values = [], [], []
    for c in range(kv_heads):
        grad_query, terms = attention_backward(
            queries, c, d_attn, *forward[c], order, count, rounded, *tables
        )
        own_terms = ring.reduced(terms)
        grad_queries.append(grad_query)
        grad_keys.append(columns(own_terms, 0))
        grad_values.append(columns(own_terms, 1))
    d_queries, d_keys, d_values = (
        jnp.concatenate(arrays, axis=1) for arrays in (grad_queries, grad_keys, grad_values)
    )
    return (projected, d_queries, d_keys, d_values)


def solution(mesh):
    placed = (
        P("seq", "head"),
        P("seq", "head"),
        P("seq", "head"),
        P("head", "seq"),
        P("seq", "head"),
        P(),
        P(),
        P("seq", None),
        P("seq", None),
        P("seq", None),
    )
    return jax.shard_map(
        on_device,
        mesh=mesh,
        in_specs=placed,
        out_specs=(P("seq", "head"), P("seq", "head"), P("seq", "head"), P("seq", "head")),
        check_vma=False,
    )
```

```python
import functools
import math

import jax
import jax.numpy as jnp
import numpy as np
from jax import lax
from jax.experimental import pallas as pl
from jax.experimental.pallas import tpu as pltpu
from jax.sharding import PartitionSpec as P

HEAD_DIMENSION = 128
BLK = 128
LOOK = 4
ANC = 2
XREF = 12
SLOTS = LOOK + ANC + XREF
GROUP = 2

neg_large = -1e30
scaling = HEAD_DIMENSION ** (-0.5)
to_base_two = scaling * math.log2(math.e)


def rows_of(index):
    return pl.ds(pl.multiple_of(index * BLK, BLK), BLK)


def product(left, right, left_dim, right_dim):
    return lax.dot_general(
        left, right, (((left_dim,), (right_dim,)), ((), ())), preferred_element_type=jnp.float32
    )


def tile_of(ref, block, head):
    return ref[
        block * BLK : (block + 1) * BLK, head * HEAD_DIMENSION : (head + 1) * HEAD_DIMENSION
    ]


def masked_scores(scores, first_slot, valid_count, heads):
    rows = heads * BLK
    key_minus_query = lax.broadcasted_iota(jnp.int32, (BLK, BLK), 1) - lax.broadcasted_iota(
        jnp.int32, (BLK, BLK), 0
    )
    ahead = jnp.concatenate([key_minus_query] * heads, axis=0)
    pieces = []
    for w in range(GROUP):
        slot = first_slot + w
        reach = jnp.where(slot < valid_count, jnp.where(slot == 0, 0, BLK), -BLK)
        piece = scores[:, w * BLK : (w + 1) * BLK]
        pieces.append(jnp.where(ahead <= reach, piece, neg_large))
    return pieces


def extended_kernel(shard_rows, section_ref, root_ref, place_ref, *refs):
    shard_refs = refs[: len(shard_rows)]
    *targets, total_ref = refs[len(shard_rows) :]
    blocks, sections = section_ref.shape[0], root_ref.shape[0]
    for number, target in enumerate(targets):
        lanes = slice(number * HEAD_DIMENSION, (number + 1) * HEAD_DIMENSION)
        for place, (shard_ref, rows) in enumerate(zip(shard_refs, shard_rows)):
            first = pl.multiple_of(place_ref[place], BLK)
            target[pl.ds(first, rows)] = shard_ref[:, lanes]
        total_ref[...] = jnp.zeros_like(total_ref)

        @pl.loop(0, blocks)
        def _(index):
            place = rows_of(section_ref[index])
            total_ref[place] += target[rows_of(index)].astype(jnp.float32)

        @pl.loop(0, sections)
        def _(index):
            target[rows_of(blocks + index)] = (
                total_ref[rows_of(index)] / root_ref[index]
            ).astype(jnp.bfloat16)


def forward_kernel(block, head, order_ref, count_ref, query_ref, keys_ref, values_ref, *refs):
    attn_ref, lse_ref, stack_ref, score_ref, wide_ref, out_ref = refs[-6:]
    heads = attn_ref.shape[1] // HEAD_DIMENSION
    for g in range(heads):
        stack_ref[g * BLK : (g + 1) * BLK] = tile_of(query_ref, block, head * heads + g)
    query = stack_ref[...]
    valid_count = count_ref[block]
    steps = (valid_count + GROUP - 1) // GROUP

    def gathered(source, step):
        return jnp.concatenate(
            [source[rows_of(order_ref[block, step * GROUP + w])] for w in range(GROUP)], axis=0
        )

    wide_ref[...] = jnp.full_like(wide_ref, neg_large)

    @pl.loop(0, steps)
    def _(step):
        scores = product(query, gathered(keys_ref, step), 1, 1)
        pieces = masked_scores(scores, step * GROUP, valid_count, heads)
        largest = wide_ref[...]
        for w, piece in enumerate(pieces):
            score_ref[step, :, w * BLK : (w + 1) * BLK] = piece
            largest = jnp.maximum(largest, piece)
        wide_ref[...] = largest

    largest = jnp.max(wide_ref[...], axis=1, keepdims=True) * to_base_two
    wide_ref[...] = jnp.zeros_like(wide_ref)

    @pl.loop(0, steps)
    def _(step):
        exponent = jnp.exp2(score_ref[step] * to_base_two - largest)
        score_ref[step] = exponent
        total = wide_ref[...]
        for w in range(GROUP):
            total = total + exponent[:, w * BLK : (w + 1) * BLK]
        wide_ref[...] = total

    total = jnp.sum(wide_ref[...], axis=1, keepdims=True)
    lse_ref[...] = jnp.broadcast_to(largest + jnp.log2(total), lse_ref.shape)
    inverse = 1.0 / total
    out_ref[...] = jnp.zeros_like(out_ref)

    @pl.loop(0, steps)
    def _(step):
        light = (score_ref[step] * inverse).astype(jnp.bfloat16)
        out_ref[...] += product(light, gathered(values_ref, step), 1, 0)

    for g in range(heads):
        attn_ref[:, g * HEAD_DIMENSION : (g + 1) * HEAD_DIMENSION] = out_ref[
            g * BLK : (g + 1) * BLK
        ].astype(jnp.bfloat16)


def backward_kernel(
    numbers, head, first, last, far,
    section_ref, root_ref, order_ref, count_ref, rounded_ref, place_ref,
    query_ref, grad_ref, keys_ref, values_ref, *refs
):
    number = len(numbers)
    *outs, query_stack, grad_stack, delta_ref, sum_ref = refs[2 * number :]
    outs = outs[-(number + 5) :] if last else outs[-(number + 2) :]
    key_sum_ref, value_sum_ref = outs[number : number + 2]
    if first:
        key_sum_ref[...] = jnp.zeros_like(key_sum_ref)
        value_sum_ref[...] = jnp.zeros_like(value_sum_ref)
    for i, block in enumerate(numbers):
        backward_block(
            block, head, order_ref, count_ref, rounded_ref,
            query_ref, grad_ref, *refs[2 * i : 2 * i + 2],
            keys_ref, values_ref, outs[i], key_sum_ref, value_sum_ref,
            query_stack, grad_stack, delta_ref, sum_ref,
        )
    if last:
        terms_ref, ahead_ref, back_ref = outs[-3:]
        blocks = section_ref.shape[0]

        @pl.loop(0, blocks)
        def _(index):
            section = section_ref[index]
            root = root_ref[section]
            for half, source in enumerate((key_sum_ref, value_sum_ref)):
                lanes = slice(half * HEAD_DIMENSION, (half + 1) * HEAD_DIMENSION)
                total = source[rows_of(index)] + source[rows_of(blocks + section)] / root
                terms_ref[rows_of(index), lanes] = total.astype(jnp.bfloat16)

        half = ahead_ref.shape[0]
        start = pl.multiple_of(place_ref[far], BLK)
        ahead_ref[...] = terms_ref[pl.ds(start, half)]
        back_ref[...] = terms_ref[pl.ds(start + half, half)]


def backward_block(
    block, head, order_ref, count_ref, rounded_ref, query_ref, grad_ref, attn_ref, lse_ref,
    keys_ref, values_ref, grad_query_ref, key_sum_ref, value_sum_ref,
    query_stack, grad_stack, delta_ref, sum_ref,
):
    heads = attn_ref.shape[1] // HEAD_DIMENSION
    for g in range(heads):
        lanes = slice(g * HEAD_DIMENSION, (g + 1) * HEAD_DIMENSION)
        rows = slice(g * BLK, (g + 1) * BLK)
        query_stack[rows] = tile_of(query_ref, block, head * heads + g)
        grad = tile_of(grad_ref, block, g)
        grad_stack[rows] = grad
        delta = jnp.sum(
            grad.astype(jnp.float32) * attn_ref[:, lanes].astype(jnp.float32), axis=1, keepdims=True
        )
        delta_ref[rows] = jnp.broadcast_to(delta, (BLK, BLK))
    query = query_stack[...]
    grad = grad_stack[...]
    valid_count = count_ref[block]
    steps = (valid_count + GROUP - 1) // GROUP
    sum_ref[...] = jnp.zeros_like(sum_ref)

    @pl.loop(0, steps)
    def _(step):
        places = [order_ref[block, step * GROUP + w] for w in range(GROUP)]
        keys = jnp.concatenate([keys_ref[rows_of(place)] for place in places], axis=0)
        values = jnp.concatenate([values_ref[rows_of(place)] for place in places], axis=0)
        scores = product(query, keys, 1, 1)
        d_weights = product(grad, values, 1, 1)
        lse = lse_ref[...]
        delta = delta_ref[...]
        light, d_scores = [], []
        for w, piece in enumerate(masked_scores(scores, step * GROUP, valid_count, heads)):
            weights = jnp.exp2(piece * to_base_two - lse)
            light.append(weights.astype(jnp.bfloat16))
            slope = d_weights[:, w * BLK : (w + 1) * BLK] - delta
            d_scores.append((weights * slope * scaling).astype(jnp.bfloat16))
        light = jnp.concatenate(light, axis=1)
        d_scores = jnp.concatenate(d_scores, axis=1)
        sum_ref[...] += product(d_scores, keys, 1, 0)
        key_terms = product(d_scores, query, 0, 0)
        value_terms = product(light, grad, 0, 0)
        for w, place in enumerate(places):
            rounds = rounded_ref[block, step * GROUP + w] > 0
            for terms, target in ((key_terms, key_sum_ref), (value_terms, value_sum_ref)):
                term = terms[w * BLK : (w + 1) * BLK]
                term = jnp.where(rounds, term.astype(jnp.bfloat16).astype(jnp.float32), term)
                target[rows_of(place)] += term

    for g in range(heads):
        grad_query_ref[:, g * HEAD_DIMENSION : (g + 1) * HEAD_DIMENSION] = sum_ref[
            g * BLK : (g + 1) * BLK
        ].astype(jnp.bfloat16)


smem = pl.BlockSpec(memory_space=pltpu.SMEM)
vmem = pl.BlockSpec(memory_space=pltpu.VMEM)
anywhere = pl.BlockSpec(memory_space=pl.ANY)


def bytes_of(*arrays):
    return sum(math.prod(array.shape) * array.dtype.itemsize for array in arrays)


def params(*arrays):
    limit = min(bytes_of(*arrays) + (20 << 20), 62 << 20)
    return pltpu.CompilerParams(vmem_limit_bytes=limit)


def extended_blocks(shards, places, block_section, root_counts):
    extended = (block_section.shape[0] + root_counts.shape[0]) * BLK
    count = shards[0].shape[1] // HEAD_DIMENSION
    outs = [jax.ShapeDtypeStruct((extended, HEAD_DIMENSION), jnp.bfloat16)] * count
    return pl.pallas_call(
        functools.partial(extended_kernel, [shard.shape[0] for shard in shards]),
        name="extended_blocks",
        in_specs=[smem] * 3 + [vmem] * len(shards),
        out_specs=[vmem] * count,
        out_shape=outs,
        scratch_shapes=[pltpu.VMEM((root_counts.shape[0] * BLK, HEAD_DIMENSION), jnp.float32)],
        compiler_params=params(*shards, *outs),
        cost_estimate=pl.CostEstimate(
            flops=bytes_of(*outs), bytes_accessed=3 * bytes_of(*outs), transcendentals=0
        ),
    )(block_section, root_counts, places, *shards)


def attention_forward(block, head, width, queries, keys, values, order, count, after):
    rows = width // HEAD_DIMENSION * BLK
    matmul = 2 * SLOTS * BLK * BLK * width
    outs = [
        jax.ShapeDtypeStruct((BLK, width), jnp.bfloat16),
        jax.ShapeDtypeStruct((rows, HEAD_DIMENSION), jnp.float32),
    ]
    scores = jax.ShapeDtypeStruct((-(-SLOTS // GROUP), rows, GROUP * BLK), jnp.float32)
    return pl.pallas_call(
        functools.partial(forward_kernel, block, head),
        name="attention_forward",
        in_specs=[smem, smem, vmem, vmem, vmem] + [anywhere] * len(after),
        out_specs=[vmem, vmem],
        out_shape=outs,
        scratch_shapes=[
            pltpu.VMEM((rows, HEAD_DIMENSION), jnp.bfloat16),
            pltpu.VMEM(scores.shape, scores.dtype),
            pltpu.VMEM((rows, HEAD_DIMENSION), jnp.float32),
            pltpu.VMEM((rows, HEAD_DIMENSION), jnp.float32),
        ],
        compiler_params=params(queries, keys, values, scores, *outs),
        cost_estimate=pl.CostEstimate(
            flops=2 * matmul, bytes_accessed=4 << 20, transcendentals=matmul // 256
        ),
    )(order, count, queries, keys, values, *after)


def attention_backward(
    numbers, head, last, ring, tables, queries, grads, forward, keys, values, sums, after
):
    number, width = len(numbers), grads.shape[1]
    rows = width // HEAD_DIMENSION * BLK
    matmul = 2 * SLOTS * BLK * BLK * width * number
    total = jax.ShapeDtypeStruct(keys.shape, jnp.float32)
    outs = [jax.ShapeDtypeStruct((BLK, width), jnp.bfloat16)] * number + [total, total]
    if last:
        tokens = queries.shape[0]
        for out_rows in (ring.size * tokens, tokens // 2, tokens // 2):
            outs.append(jax.ShapeDtypeStruct((out_rows, 2 * HEAD_DIMENSION), jnp.bfloat16))
    arrays = [queries, grads, keys, values, *[array for pair in forward for array in pair]]
    first_sum = len(tables) + len(arrays) + len(after)
    return pl.pallas_call(
        functools.partial(backward_kernel, numbers, head, not sums, last, ring.terms_at(ring.size // 2)),
        name="attention_backward",
        in_specs=[smem] * len(tables)
        + [vmem] * len(arrays)
        + [anywhere] * len(after)
        + [vmem] * len(sums),
        out_specs=[vmem] * len(outs),
        out_shape=outs,
        input_output_aliases={first_sum + i: number + i for i in range(len(sums))},
        scratch_shapes=[
            pltpu.VMEM((rows, HEAD_DIMENSION), jnp.bfloat16),
            pltpu.VMEM((rows, HEAD_DIMENSION), jnp.bfloat16),
            pltpu.VMEM((rows, HEAD_DIMENSION), jnp.float32),
            pltpu.VMEM((rows, HEAD_DIMENSION), jnp.float32),
        ],
        compiler_params=params(*arrays, *outs, *sums),
        cost_estimate=pl.CostEstimate(
            flops=5 * matmul, bytes_accessed=number * (4 << 20), transcendentals=matmul // 256
        ),
    )(*tables, *arrays, *after, *sums)


class Ring:
    def __init__(self, axis, key_rows, weight_rows):
        self.axis = axis
        self.size = size = lax.axis_size(axis)
        self.cycle = cycle = [*range(0, size, 2), *reversed(range(1, size, 2))]
        distances = [0]
        for step in range(1, size // 2):
            distances += [-step, step]
        table = np.zeros((size, 0), np.int32)
        at = np.argsort(np.array(cycle))
        cycle = np.array(cycle)
        for rows in (key_rows, weight_rows):
            whole = np.stack([cycle[(at + distance) % size] * rows for distance in distances], 1)
            far = cycle[(at + size // 2) % size][:, None] * rows + np.array([[0, rows // 2]])
            table = np.concatenate([table, whole, far], axis=1)
        self.key_places, self.weight_places = 0, size + 1
        self.term_places = table.shape[1]
        terms = np.stack([cycle[(at + distance) % size] * key_rows for distance in range(size)], 1)
        table = np.concatenate([table, terms], axis=1).astype(np.int32)
        row = lax.dynamic_slice_in_dim(jnp.asarray(table), lax.axis_index(axis), 1)
        self.places = row.reshape(-1)

    def terms_at(self, distance):
        return self.term_places + distance % self.size

    def sent(self, block, direction):
        cycle, size = self.cycle, self.size
        route = [(cycle[k], cycle[(k + direction) % size]) for k in range(size)]
        return lax.ppermute(block, self.axis, route)

    def gather(self, block):
        return Gather(self, block)


class Gather:
    def __init__(self, ring, block):
        self.ring = ring
        self.half = block.shape[0] // 2
        self.pieces = [block]
        self.ahead = self.back = block
        self.left = ring.size // 2

    def step(self, after=()):
        ahead, back = self.ahead, self.back
        if after:
            ahead, back, _ = lax.optimization_barrier((ahead, back, list(after)))
        self.left -= 1
        if not self.left:
            ahead, back = ahead[: self.half], back[self.half :]
        self.ahead, self.back = self.ring.sent(ahead, 1), self.ring.sent(back, -1)
        self.pieces += [self.ahead, self.back]
        return [self.ahead, self.back]

    def rest(self, after=()):
        while self.left:
            self.step(after)
        return self.pieces


def added_kernel(up, down, place_ref, terms_ref, ahead_in, back_in, *refs):
    ahead_ref, back_ref = refs[-2:]
    rows, half = ahead_ref.shape[0], ahead_in.shape[0]
    for place, source, target, first in (
        (up, ahead_in, ahead_ref, 0), (down, back_in, back_ref, rows - half)
    ):
        start = pl.multiple_of(place_ref[place], BLK)
        if half < rows:
            target[...] = terms_ref[pl.ds(start, rows)]
        own = terms_ref[pl.ds(start + first, half)].astype(jnp.float32)
        target[first : first + half] = (own + source[...].astype(jnp.float32)).astype(jnp.bfloat16)


def added_terms(ring, step, terms, ahead, back, after):
    out = jax.ShapeDtypeStruct((terms.shape[0] // ring.size, terms.shape[1]), jnp.bfloat16)
    return pl.pallas_call(
        functools.partial(added_kernel, ring.terms_at(step), ring.terms_at(-step)),
        name="added_terms",
        in_specs=[smem] + [vmem] * 3 + [anywhere] * len(after),
        out_specs=[vmem, vmem],
        out_shape=[out, out],
        compiler_params=params(terms, ahead, back, out, out),
        cost_estimate=pl.CostEstimate(
            flops=out.size, bytes_accessed=bytes_of(out, out, out), transcendentals=0
        ),
    )(ring.places, terms, ahead, back, *after)


class Reduction:
    def __init__(self, ring, terms, ahead, back):
        self.ring, self.terms = ring, terms
        self.moves = [ring.sent(ahead, 1), ring.sent(back, -1)]
        self.left = ring.size // 2 - 1

    def step(self, after=()):
        summed = added_terms(self.ring, self.left, self.terms, *self.moves, after)
        self.left -= 1
        self.moves = [self.ring.sent(summed[0], 1), self.ring.sent(summed[1], -1)]
        return list(summed)

    def rest(self):
        while self.left:
            self.step()
        return self.moves


def last_kernel(own, place_ref, *refs):
    d_keys_ref, d_values_ref = refs[-2:]
    start = pl.multiple_of(place_ref[own], BLK)
    for c in range(len(refs) // 3):
        terms_ref, ahead_ref, back_ref = refs[3 * c : 3 * c + 3]
        total = terms_ref[pl.ds(start, ahead_ref.shape[0])].astype(jnp.float32)
        total = total + ahead_ref[...].astype(jnp.float32) + back_ref[...].astype(jnp.float32)
        lanes = slice(c * HEAD_DIMENSION, (c + 1) * HEAD_DIMENSION)
        d_keys_ref[:, lanes] = total[:, :HEAD_DIMENSION].astype(jnp.bfloat16)
        d_values_ref[:, lanes] = total[:, HEAD_DIMENSION:].astype(jnp.bfloat16)


def last_sums(ring, arrays):
    out = jax.ShapeDtypeStruct(
        (arrays[1].shape[0], len(arrays) // 3 * HEAD_DIMENSION), jnp.bfloat16
    )
    return pl.pallas_call(
        functools.partial(last_kernel, ring.terms_at(0)),
        name="last_sums",
        in_specs=[smem] + [vmem] * len(arrays),
        out_specs=[vmem, vmem],
        out_shape=[out, out],
        compiler_params=params(*arrays, out, out),
        cost_estimate=pl.CostEstimate(
            flops=4 * out.size, bytes_accessed=4 * bytes_of(out, out), transcendentals=0
        ),
    )(ring.places, *arrays)


def key_slots(block_section, section_parent, xref_owner, xref_block, xref_valid, first_blk):
    blocks = block_section.shape[0]
    blk_count = xref_block.shape[0]
    own = first_blk + jnp.arange(blk_count, dtype=jnp.int32)
    offsets = jnp.concatenate([jnp.array([0], jnp.int32), jnp.arange(1 - LOOK, 0, dtype=jnp.int32)])
    window = own[:, None] + offsets[None, :]
    is_block = jnp.arange(blocks, dtype=jnp.int32)

    def section_of(index):
        return jnp.sum(
            jnp.where(index[..., None] == is_block, block_section + 1, 0), axis=-1
        ) - 1

    my_sec = section_of(own)
    window_ok = section_of(window) == my_sec[:, None]
    chain = [my_sec]
    is_section = jnp.arange(section_parent.shape[0], dtype=jnp.int32)
    for _ in range(ANC - 1):
        prior = chain[-1]
        chain.append(
            jnp.sum(jnp.where(prior[:, None] == is_section, section_parent + 1, 0), axis=1) - 1
        )
    ancestors = jnp.stack(chain, axis=1)
    targets = xref_owner.reshape(blk_count, XREF) * blk_count + xref_block
    place = jnp.concatenate(
        [jnp.maximum(window, 0), blocks + jnp.maximum(ancestors, 0), targets], axis=1
    )
    valid = jnp.concatenate([window_ok, ancestors >= 0, xref_valid > 0], axis=1)
    slot = jnp.arange(SLOTS, dtype=jnp.int32)
    earlier = slot[:, None] < slot[None, :]
    before = jnp.sum(jnp.where(earlier[None], valid[:, :, None].astype(jnp.int32), 0), axis=1)
    count = jnp.sum(valid.astype(jnp.int32), axis=1)
    rank = jnp.where(valid, before, count[:, None] + slot - before)
    sorted_from = rank[:, :, None] == slot
    padded = -(-SLOTS // GROUP) * GROUP - SLOTS
    order = jnp.sum(jnp.where(sorted_from, place[:, :, None], 0), axis=1)
    is_ref = (slot >= LOOK + ANC).astype(jnp.int32)
    rounded = jnp.sum(jnp.where(sorted_from, is_ref[None, :, None], 0), axis=1)
    order, rounded = (jnp.pad(table, ((0, 0), (0, padded))) for table in (order, rounded))
    return order, rounded, count


def exchanged(block, axis, bit):
    size = lax.axis_size(axis)
    return lax.ppermute(block, axis, [(i, i ^ bit) for i in range(size)])


def exchange_order(axis):
    order, bit = [0], lax.axis_size(axis) // 2
    while bit:
        order += [index ^ bit for index in order]
        bit //= 2
    return order


def gathered_by_exchange(block, axis, after):
    parts, bit = [block], lax.axis_size(axis) // 2
    while bit:
        parts += [exchanged(part, axis, bit) for part in parts]
        bit //= 2
        if bit:
            parts = [held(part, after) for part in parts]
    return parts


def reduced_by_exchange(parts, axis, bit):
    while bit < lax.axis_size(axis):
        half = parts.shape[0] // 2
        given = exchanged(parts[half:], axis, bit)
        parts = (parts[:half].astype(jnp.float32) + given.astype(jnp.float32)).astype(jnp.bfloat16)
        bit *= 2
    return parts[0]


def held(array, after):
    return lax.optimization_barrier((array, after))[0]


def cotangent_kernel(shard_rows, order, base, me_ref, place_ref, *refs):
    out_ref, weight_ref = refs[-2:]
    parts, refs = refs[: len(order)], refs[len(order) :]
    part_width = parts[0].shape[1]
    for number, rows in enumerate(shard_rows):
        first = pl.multiple_of(place_ref[base + number], 16)
        weight_ref[pl.ds(first, rows)] = refs[number][...]
    total = None
    for part_ref, index in zip(parts, order):
        first = pl.multiple_of((me_ref[0] ^ index) * part_width, 16)
        term = product(part_ref[...], weight_ref[pl.ds(first, part_width)], 1, 0)
        total = term if total is None else total + term
    out_ref[...] = total.astype(jnp.bfloat16)


def cotangent_of_attn(parts, shards, ring, me, order, after):
    count, (tokens, part_width) = len(parts), parts[0].shape
    width = shards[0].shape[1]
    outs = [
        jax.ShapeDtypeStruct((tokens, width), jnp.bfloat16),
        jax.ShapeDtypeStruct((count * part_width, width), jnp.bfloat16),
    ]
    return pl.pallas_call(
        functools.partial(
            cotangent_kernel, [shard.shape[0] for shard in shards], order, ring.weight_places
        ),
        name="cotangent_of_attn",
        in_specs=[smem, smem] + [vmem] * (count + len(shards)) + [anywhere] * len(after),
        out_specs=[vmem, vmem],
        out_shape=outs,
        compiler_params=params(*parts, *shards, *outs),
        cost_estimate=pl.CostEstimate(
            flops=2 * count * tokens * part_width * width,
            bytes_accessed=bytes_of(*parts, *outs, *outs),
            transcendentals=0,
        ),
    )(me, ring.places, *parts, *shards, *after)


def projection_kernel(order, kv_heads, added, waits, me_ref, *refs):
    *refs, out_ref = refs
    refs = refs[waits:]
    if added:
        *refs, added_ref = refs
    part_width = out_ref.shape[2]
    weights, attns = refs[:kv_heads], refs[kv_heads:]
    blocks = len(attns) // kv_heads
    for j, index in enumerate(order):
        first = pl.multiple_of((me_ref[0] ^ index) * part_width, 16)
        for c, weight_ref in enumerate(weights):
            attn = jnp.concatenate([ref[...] for ref in attns[c * blocks : (c + 1) * blocks]], axis=0)
            term = product(attn, weight_ref[pl.ds(first, part_width)], 1, 1)
            total = term if c == 0 else total + term
        if added:
            total = total + added_ref[j].astype(jnp.float32)
        out_ref[j] = total.astype(jnp.bfloat16)


def projection_parts(attns, weights, me, order, after, added=()):
    kv_heads = len(weights)
    width, count = weights[0].shape[1], 2 * len(order)
    tokens = len(attns) // kv_heads * BLK
    part_width = weights[0].shape[0] // count
    out = jax.ShapeDtypeStruct((len(order), tokens, part_width), jnp.bfloat16)
    return pl.pallas_call(
        functools.partial(projection_kernel, order, kv_heads, bool(added), len(after)),
        name="projection_parts",
        in_specs=[smem]
        + [anywhere] * len(after)
        + [vmem] * (kv_heads + len(attns) + len(added)),
        out_specs=vmem,
        out_shape=out,
        compiler_params=params(*weights, *attns, *added, out),
        cost_estimate=pl.CostEstimate(
            flops=2 * len(order) * tokens * part_width * width * kv_heads,
            bytes_accessed=bytes_of(out, *weights, *attns),
            transcendentals=0,
        ),
    )(me, *after, *weights, *attns, *added)


def on_device(
    queries,
    keys,
    values,
    out_weight,
    d_proj,
    block_section,
    section_parent,
    xref_owner,
    xref_block,
    xref_valid,
):
    blk_count = queries.shape[0] // BLK
    kv_heads = keys.shape[1] // HEAD_DIMENSION
    width = queries.shape[1] // kv_heads
    pieces = range(blk_count)
    first_blk = lax.axis_index("seq") * blk_count
    me = lax.axis_index("head").reshape(1)

    def columns(array, index, size=HEAD_DIMENSION):
        return array[:, index * size : (index + 1) * size]

    ring = Ring("seq", keys.shape[0], out_weight.shape[1])
    section_ids = jnp.arange(section_parent.shape[0], dtype=jnp.int32)
    root_counts = jnp.sqrt(
        jnp.sum((block_section[:, None] == section_ids[None, :]).astype(jnp.float32), axis=0)
    )
    order, rounded, count = key_slots(
        block_section, section_parent, xref_owner, xref_block, xref_valid, first_blk
    )
    weight = [columns(out_weight.T, c, width) for c in range(kv_heads)]
    gather = ring.gather(
        jnp.concatenate(
            [columns(array, c) for c in range(kv_heads) for array in (keys, values)], axis=1
        )
    )
    came = gather.step()
    shards = gather.rest([order, rounded, count, root_counts, ring.places, *weight, *came])
    gathers = [ring.gather(weight[c]) for c in range(kv_heads)]
    d_parts = gathered_by_exchange(d_proj, "head", shards[-1])
    extended = extended_blocks(shards, ring.places, block_section, root_counts)
    blocks = [extended[2 * c : 2 * c + 2] for c in range(kv_heads)]

    forward = [[] for _ in range(kv_heads)]
    total = kv_heads * blk_count
    came, done = gathers[0].step(shards[-2:]), []
    steps = gathers[0].left + 1
    taken = 1
    for number in range(total):
        c, b = divmod(number, blk_count)
        ready = []
        while taken < steps and number * steps >= taken * total:
            ready = came
            came = gathers[0].step(done)
            taken += 1
        out = attention_forward(b, c, width, queries, *blocks[c], order, count, [*ready, *done])
        forward[c].append(out)
        done = [out[0]]

    parts_order = exchange_order("head")
    half = len(parts_order) // 2
    attns = [forward[c][b][0] for c in range(kv_heads) for b in pieces]
    sums_bytes = 4 * bytes_of(jax.ShapeDtypeStruct(blocks[0][0].shape, jnp.float32))
    span = 1 if sums_bytes < (30 << 20) else blk_count
    tables = (block_section, root_counts, order, count, rounded, ring.places)
    d_queries, last_arrays, weight_rows = [], [], []
    reducing = None
    for c in range(kv_heads):
        following = gathers[c + 1] if c + 1 < kv_heads else None
        if following:
            came = following.step(gathers[c].pieces[-4:-2])
            steps, taken = following.left + 1, 1
        grad, rows = cotangent_of_attn(d_parts, gathers[c].rest(), ring, me, parts_order, done)
        weight_rows.append(rows)
        done = [grad]
        sums, grad_query = [], []
        for b in range(0, blk_count, span):
            ready = []
            if following and taken < steps:
                ready = came
                came = following.step(done)
                taken += 1
            if reducing and reducing.left > 1:
                ready = [*ready, *reducing.step(done)]
            last = b + span == blk_count
            numbers = list(range(b, b + span))
            out = attention_backward(
                numbers, c, last, ring, tables, queries, grad,
                [forward[c][i] for i in numbers], *blocks[c], sums, ready,
            )
            grad_query += out[:span]
            sums = out[span : span + 2]
            done = [out[0]]
        terms, ahead, back = out[-3:]
        if reducing:
            last_arrays += [reducing.terms, *reducing.rest()]
        reducing = Reduction(ring, terms, ahead, back)
        d_queries.append(jnp.concatenate(grad_query, axis=0))

    given = projection_parts(attns, weight_rows, me, parts_order[half:], [terms])
    summed = reducing.step([given])
    kept = projection_parts(
        attns, weight_rows, me, parts_order[:half], summed, [exchanged(given, "head", 1)]
    )
    reducing.step([kept])
    last_arrays += [reducing.terms, *reducing.rest()]
    projected = reduced_by_exchange(kept, "head", 2)
    return (projected, jnp.concatenate(d_queries, axis=1), *last_sums(ring, last_arrays))


def solution(mesh):
    placed = (
        P("seq", "head"),
        P("seq", "head"),
        P("seq", "head"),
        P("head", "seq"),
        P("seq", "head"),
        P(),
        P(),
        P("seq", None),
        P("seq", None),
        P("seq", None),
    )
    return jax.shard_map(
        on_device,
        mesh=mesh,
        in_specs=placed,
        out_specs=(P("seq", "head"), P("seq", "head"), P("seq", "head"), P("seq", "head")),
        check_vma=False,
    )
```
